32 devices in a mesh: groups: 2 (over x), dp: 16 (over z, y, core).
Axes of the slice: x: 2, y: 2, z: 4, core: 2. Of those that a mesh axis runs over, the one named last changes fastest.
Arguments:
- images: bfloat16 [16, 128, 128, 320], P('groups', 'dp'), parts along dimension 0, may hold values from -6 to 6
- kernel_weights: bfloat16 [16, 2, 3, 3, 320, 320], P('dp'), may hold values from -0.109375 to 0.109375
- kernel_momentum: float32 [16, 2, 3, 3, 320, 320], P('dp'), may hold values from -0.12 to 0.12
- kernel_grads: bfloat16 [16, 2, 3, 3, 320, 320], P('dp'), may hold values from -0.119628906 to 0.119628906
- owners: int32 [2], replicated, may hold values from 0 to 15
Outputs:
- blocks_out: bfloat16 [16, 128, 128, 320], P('groups', 'dp'), parts along dimension 0
The draws below stay inside these ranges and needn't reach their ends.
There are 2 independent parts, one for each index of `groups`. The reference program is written for one: setup_inputs(seed, part) draws one part's arguments, and reference() takes and returns one part's arrays. A program takes and returns all parts, laid end to end along the dimension named above; an argument that names none is the same for every part. Nothing has to cross between parts.
Inputs may be any that keep to these rules, and one draw needn't show every extreme that they name: `owners`: each entry is a slot index along the first dimension of the kernel state.
All inputs are finite; a program needn't handle non-finite values.
Results may differ from the reference program's by a relative error of at most 0.0095.
Values may be sent and summed in bfloat16 or wider, within the bound.
A program may use at most 128 MiB of HBM per device.

```python
import jax
import jax.numpy as jnp
from jax import lax

C = 320
IMGS = 8
WIDTH = 128
HEIGHT = 128
N_DP = 16


def level_of(own_key, dims, shards, low, high):
    level = 1.0
    for axis_at, blocks in shards:
        steps = jax.random.uniform(jax.random.fold_in(jax.random.fold_in(own_key, 6), axis_at), (blocks,), jnp.float32, low / len(shards), high / len(shards))
        level = level * jnp.repeat(jnp.exp(steps), dims[axis_at] // blocks).reshape((-1,) + (1,) * (len(dims) - 1 - axis_at))
    return level


def centred(own_key, dims, scale, most, shards=(), kind=jnp.bfloat16):
    gain = level_of(own_key, dims, shards, -0.22, 0.18) if shards else 1.0
    result = jax.random.normal(own_key, dims, jnp.float32) * scale * gain
    return jnp.minimum(jnp.maximum(result, -most), most).astype(kind)


def setup_inputs(seed: int = 0, part: int = 0) -> dict:
    keys = jax.random.split(jax.random.key(seed), 6)
    part_splits = jax.random.split(jax.random.fold_in(keys[5], part), 6)
    return {
        "images": centred(part_splits[0], (IMGS, HEIGHT, WIDTH, C), 1.0, 6.0, ((1, 16),)),
        "kernel_weights": centred(keys[1], (N_DP, 2, 3, 3, C, C), (9 * C) ** -0.5, 0.109375, ((0, 16),)),
        "kernel_momentum": centred(keys[2], (N_DP, 2, 3, 3, C, C), 0.02, 0.12, ((0, 16),), jnp.float32),
        "kernel_grads": centred(keys[3], (N_DP, 2, 3, 3, C, C), 0.02, 0.119628906, ((0, 16),)),
        "owners": jax.random.randint(keys[4], (2,), 0, N_DP).astype(jnp.int32),
    }


momentum_decay = 0.9
learn_rate = 0.5


def convolve(activated, kernel):
    return lax.conv_general_dilated(activated, kernel, (1, 1), ((1, 1), (1, 1)), dimension_numbers=("NHWC", "HWIO", "NHWC"), preferred_element_type=jnp.float32)


def reference(images, kernel_weights, kernel_momentum, kernel_grads, owners):
    kernels = []
    for kernel_index in range(2):
        slot = owners[kernel_index]
        velocity = momentum_decay * kernel_momentum[slot, kernel_index] + kernel_grads[slot, kernel_index].astype(jnp.float32)
        updated = kernel_weights[slot, kernel_index].astype(jnp.float32) - learn_rate * velocity
        kernels.append(updated.astype(jnp.bfloat16))
    activated = jax.nn.silu(images.astype(jnp.float32)).astype(jnp.bfloat16)
    hidden = (images.astype(jnp.float32) + convolve(activated, kernels[0])).astype(jnp.bfloat16)
    activated = jax.nn.silu(hidden.astype(jnp.float32)).astype(jnp.bfloat16)
    return (hidden.astype(jnp.float32) + convolve(activated, kernels[1])).astype(jnp.bfloat16)
```

```python
import functools

import jax
import jax.numpy as jnp
from jax import lax
from jax.experimental import pallas as pl
from jax.experimental.pallas import tpu as pltpu
from jax.sharding import PartitionSpec as P

momentum_decay = 0.9
learn_rate = 0.5
MESH = pl.DeviceIdType.MESH
hop = 2


def spread_kernel(
    groups, depth, chunks, mask_ref, w_hbm, m_hbm, g_hbm, out_ref,
    w_buf, m_buf, g_buf, own, pair_out, pair_in, col, col_in, joined, fwd, fwd_in, back, back_in,
    load_sem, pair_sem, col_sem, fwd_sem, back_sem, mate_sem, cross_sem, pass_sem,
):
    group, at = lax.axis_index("groups"), lax.axis_index("dp")
    z, y, core = at // 4, (at // 2) % 2, at % 2
    mate = at + 1 - 2 * core
    across = at + 2 - 4 * y
    share = 2 * group + core
    last = depth - 1

    def loads(k):
        src = pl.ds(2 * group, 2)
        return [
            pltpu.make_async_copy(ref.at[k, src], buf.at[k], load_sem.at[i, k])
            for i, (ref, buf) in enumerate(((w_hbm, w_buf), (m_hbm, m_buf), (g_hbm, g_buf)))
        ]

    def remote(src, dst, sem, k, **where):
        return pltpu.make_async_remote_copy(
            src, dst, sem.at[0, k], sem.at[1, k], device_id=where, device_id_type=MESH
        )

    def to_pair(k):
        return remote(pair_out.at[k], pair_in.at[k], pair_sem, k, dp=mate)

    def to_col(k):
        return remote(col.at[k], col_in.at[k], col_sem, k, dp=across)

    def to_fwd(k, up=4):
        return remote(fwd.at[k], fwd_in.at[k], fwd_sem, k, dp=at + up)

    def to_back(k, down=4):
        return remote(back.at[k], back_in.at[k], back_sem, k, dp=at - down)

    def to_mate(k):
        return remote(out_ref.at[k, share], out_ref.at[k, share], mate_sem, k, dp=mate)

    others = [lax.rem(group + step, groups) for step in range(1, groups)]

    def to_cross(k, i):
        return remote(
            out_ref.at[k, share], out_ref.at[k, share], cross_sem.at[i], k, groups=others[i]
        )

    def from_cross(k, i):
        sent_by = lax.rem(group + groups - 1 - i, groups)
        slot = 2 * sent_by + core
        return pltpu.make_async_remote_copy(
            out_ref.at[k, slot], out_ref.at[k, slot], cross_sem.at[i, 0, k], cross_sem.at[i, 1, k],
            device_id={"groups": others[i]}, device_id_type=MESH,
        )

    def to_pass(k, i):
        slot = 2 * lax.rem(group + groups - 1 - i, groups) + core
        return remote(out_ref.at[k, slot], out_ref.at[k, slot], pass_sem.at[i], k, dp=mate)

    def start_loads(k, carry):
        for copy in loads(k):
            copy.start()
        return carry

    lax.fori_loop(0, chunks, start_loads, 0)

    barrier = pltpu.get_barrier_semaphore()
    pl.semaphore_signal(barrier, inc=1, device_id={"dp": mate}, device_id_type=MESH)
    pl.semaphore_signal(barrier, inc=1, device_id={"dp": across}, device_id_type=MESH)
    for other in others:
        pl.semaphore_signal(barrier, inc=1, device_id={"groups": other}, device_id_type=MESH)

    @pl.when(z > 0)
    def _():
        pl.semaphore_signal(barrier, inc=1, device_id={"dp": at - 4}, device_id_type=MESH)

    @pl.when(z < last)
    def _():
        pl.semaphore_signal(barrier, inc=1, device_id={"dp": at + 4}, device_id_type=MESH)

    ahead, behind = jnp.where(z < last, 1, 0), jnp.where(z > 0, 1, 0)
    pl.semaphore_wait(barrier, 1 + groups + ahead + behind)

    def at_step(k, what):
        pl.when((k >= 0) & (k < chunks))(lambda: what(k))

    def renew(k):
        for copy in loads(k):
            copy.wait()
        mine = mask_ref[k] > 0.5

        def new(c):
            velocity = momentum_decay * m_buf[k, c] + g_buf[k, c].astype(jnp.float32)
            updated = w_buf[k, c].astype(jnp.float32) - learn_rate * velocity
            return jnp.where(mine, updated, 0.0).astype(jnp.bfloat16)

        pair_out[k] = new(1 - core)
        to_pair(k).start()
        own[k] = new(core)

    def join_pair(k):
        to_pair(k).wait_recv()
        col[k] = own[k] + pair_in[k]
        to_col(k).start()

    def join_col(k):
        to_col(k).wait_recv()
        joined[k] = col[k] + col_in[k]

    def go_fwd(k):
        @pl.when(z == 0)
        def _():
            fwd[k] = joined[k]

        @pl.when(z > 0)
        def _():
            to_fwd(k, -4).wait_recv()
            fwd[k] = joined[k] + fwd_in[k]

        @pl.when(z < last)
        def _():
            to_fwd(k).start()

    def go_back(k):
        @pl.when(z == last)
        def _():
            back[k] = joined[k]

        @pl.when(z < last)
        def _():
            to_back(k, -4).wait_recv()
            back[k] = joined[k] + back_in[k]

        @pl.when(z > 0)
        def _():
            to_back(k).start()

    def finish(k):
        @pl.when(z < last)
        def _():
            out_ref[k, share] = fwd[k] + back_in[k]

        @pl.when(z == last)
        def _():
            out_ref[k, share] = fwd[k]

        to_mate(k).start()
        for i in range(groups - 1):
            to_cross(k, i).start()

    def pass_on(k):
        for i in range(groups - 1):
            from_cross(k, i).wait_recv()
            to_pass(k, i).start()

    def step(t, carry):
        at_step(t, renew)
        at_step(t - 1, join_pair)
        begin = 1 + hop
        at_step(t - begin, join_col)
        at_step(t - begin - z * hop, go_fwd)
        at_step(t - begin - (last - z) * hop, go_back)
        at_step(t - begin - last * hop, finish)
        at_step(t - begin - last * hop - hop, pass_on)
        return carry

    lax.fori_loop(0, chunks + 1 + hop + last * hop + hop, step, 0)

    def drain(k, carry):
        to_pair(k).wait_send()
        to_col(k).wait_send()

        @pl.when(z < last)
        def _():
            to_fwd(k).wait_send()

        @pl.when(z > 0)
        def _():
            to_back(k).wait_send()

        to_mate(k).wait()
        for i in range(groups - 1):
            to_cross(k, i).wait_send()
            to_pass(k, i).wait()
        return carry

    lax.fori_loop(0, chunks, drain, 0)


def spread(kernel_weights, kernel_momentum, kernel_grads, owners):
    groups, dp = lax.axis_size("groups"), lax.axis_size("dp")
    _, kernels, rows, columns, fan_in, fan_out = kernel_weights.shape
    chunks, shares = kernels * rows * columns, 2 * groups
    part = fan_in // shares
    cut = lambda a: a.reshape(chunks, shares, part, fan_out)
    mine = (owners == lax.axis_index("dp")).astype(jnp.float32)
    mask = jnp.broadcast_to(
        jnp.repeat(mine, rows * columns)[:, None, None], (chunks, 1, fan_out)
    )
    piece = pltpu.VMEM((chunks, part, fan_out), jnp.bfloat16)
    load = lambda dtype: pltpu.VMEM((chunks, 2, part, fan_out), dtype)
    sems = pltpu.SemaphoreType.DMA((2, chunks))
    many = pltpu.SemaphoreType.DMA((groups - 1, 2, chunks))
    out = pl.pallas_call(
        functools.partial(spread_kernel, groups, dp // 4, chunks),
        out_shape=jax.ShapeDtypeStruct((chunks, shares, part, fan_out), jnp.bfloat16),
        in_specs=[pl.BlockSpec(memory_space=pltpu.VMEM)] + [pl.BlockSpec(memory_space=pl.ANY)] * 3,
        out_specs=pl.BlockSpec(memory_space=pltpu.VMEM),
        scratch_shapes=[load(jnp.bfloat16), load(jnp.float32), load(jnp.bfloat16)]
        + [piece] * 10
        + [pltpu.SemaphoreType.DMA((3, chunks)), sems, sems, sems, sems, sems, many, many],
        compiler_params=pltpu.CompilerParams(
            collective_id=0, has_side_effects=True, vmem_limit_bytes=56 << 20
        ),
    )(mask, cut(kernel_weights), cut(kernel_momentum), cut(kernel_grads))
    return out.reshape(kernels, rows, columns, fan_in, fan_out)


def silu(v):
    return v / (1.0 + jnp.exp(-v))


def conv_kernel(x_ref, top_ref, bottom_ref, k_ref, o_ref, patch, wide, rest):
    height, width, channels = x_ref.shape[1:]
    full = channels // 128 // 2 * 256
    tail = channels - full
    reach = 3 * channels
    span = patch.shape[-1]

    @pl.when(pl.program_id(0) == 0)
    def _():
        patch[:, :, reach:] = jnp.zeros((height + 2, width, span - reach), jnp.bfloat16)
        rest[reach:, :] = jnp.zeros((span - reach, rest.shape[1]), jnp.bfloat16)
        for dr in range(3):
            base = dr * span
            wide[base + reach : base + span, :] = jnp.zeros((span - reach, full), jnp.bfloat16)
            for dc in range(3):
                low, high = dc * full, 3 * full + dc * tail
                lanes = slice(dr * tail, (dr + 1) * tail)
                wide[base + low : base + low + full, :] = k_ref[dr, dc, :full, :full]
                wide[base + high : base + high + tail, :] = k_ref[dr, dc, full:, :full]
                rest[low : low + full, lanes] = k_ref[dr, dc, :full, full:]
                rest[high : high + tail, lanes] = k_ref[dr, dc, full:, full:]

    column = lax.broadcasted_iota(jnp.int32, (width, 1), 0)
    for row in range(height + 2):
        if row == 0:
            v = top_ref[0, 0]
        elif row == height + 1:
            v = bottom_ref[0, 0]
        else:
            v = x_ref[0, row - 1]
        a = silu(v.astype(jnp.float32))
        before = jnp.where(column == 0, 0.0, pltpu.roll(a, 1, 0)).astype(jnp.bfloat16)
        after = jnp.where(column == width - 1, 0.0, pltpu.roll(a, width - 1, 0)).astype(jnp.bfloat16)
        for dc, part in enumerate((before, a.astype(jnp.bfloat16), after)):
            patch[row, :, dc * full : (dc + 1) * full] = part[:, :full]
            high = 3 * full + dc * tail
            patch[row, :, high : high + tail] = part[:, full:]

    cells = height * width
    lhs = jnp.concatenate(
        [patch[dr : dr + height].reshape(cells, span) for dr in range(3)], axis=-1
    )
    main = jnp.dot(lhs, wide[...], preferred_element_type=jnp.float32)
    side = jnp.dot(
        patch[...].reshape((height + 2) * width, span), rest[...], preferred_element_type=jnp.float32
    )
    side = (
        side[:cells, :tail]
        + side[width : width + cells, tail : 2 * tail]
        + side[2 * width : 2 * width + cells, 2 * tail : 3 * tail]
    )
    x = x_ref[0].reshape(cells, channels)
    o_ref[0, :, :, :full] = (
        (x[:, :full].astype(jnp.float32) + main).astype(o_ref.dtype).reshape(height, width, full)
    )
    o_ref[0, :, :, full:] = (
        (x[:, full:].astype(jnp.float32) + side).astype(o_ref.dtype).reshape(height, width, tail)
    )


def residual_conv(x, kernel):
    images, height, width, channels = x.shape
    count = lax.axis_size("dp")
    top = lax.ppermute(x[:, -1:], "dp", [(i, i + 1) for i in range(count - 1)])
    bottom = lax.ppermute(x[:, :1], "dp", [(i + 1, i) for i in range(count - 1)])
    full = channels // 128 // 2 * 256
    tail = channels - full
    span = -(-3 * channels // 256) * 256
    image = pl.BlockSpec((1, height, width, channels), lambda i: (i, 0, 0, 0))
    edge = pl.BlockSpec((1, 1, width, channels), lambda i: (i, 0, 0, 0))
    return pl.pallas_call(
        conv_kernel,
        out_shape=jax.ShapeDtypeStruct(x.shape, x.dtype),
        grid=(images,),
        in_specs=[image, edge, edge, pl.BlockSpec(kernel.shape, lambda i: (0, 0, 0, 0))],
        out_specs=image,
        scratch_shapes=[
            pltpu.VMEM((height + 2, width, span), jnp.bfloat16),
            pltpu.VMEM((3 * span, full), jnp.bfloat16),
            pltpu.VMEM((span, 3 * tail), jnp.bfloat16),
        ],
        compiler_params=pltpu.CompilerParams(vmem_limit_bytes=56 << 20),
    )(x, top, bottom, kernel)


def local(images, kernel_weights, kernel_momentum, kernel_grads, owners):
    kernels = spread(kernel_weights, kernel_momentum, kernel_grads, owners)
    hidden = residual_conv(images, kernels[0])
    return residual_conv(hidden, kernels[1])


def solution(mesh):
    placed = (
        P("groups", "dp", None, None),
        P("dp", None, None, None, None, None),
        P("dp", None, None, None, None, None),
        P("dp", None, None, None, None, None),
        P(),
    )
    return jax.shard_map(
        local, mesh=mesh, in_specs=placed, out_specs=P("groups", "dp", None, None), check_vma=False
    )
```

```python
import functools

import jax
import jax.numpy as jnp
from jax import lax
from jax.experimental import pallas as pl
from jax.experimental.pallas import tpu as pltpu
from jax.sharding import PartitionSpec as P

momentum_decay = 0.9
learn_rate = 0.5
MESH = pl.DeviceIdType.MESH
hop = 2


def spread_kernel(
    groups, depth, chunks, mask_ref, w_hbm, m_hbm, g_hbm, out_ref,
    w_buf, m_buf, g_buf, own, pair_out, pair_in, col, col_in, joined, fwd, fwd_in, back, back_in,
    load_sem, pair_sem, col_sem, fwd_sem, back_sem, mate_sem, cross_sem, pass_sem,
):
    group, at = lax.axis_index("groups"), lax.axis_index("dp")
    z, y, core = at // 4, (at // 2) % 2, at % 2
    mate = at + 1 - 2 * core
    across = at + 2 - 4 * y
    share = 2 * group + core
    last = depth - 1

    def loads(k):
        src = pl.ds(2 * group, 2)
        return [
            pltpu.make_async_copy(ref.at[k, src], buf.at[k], load_sem.at[i, k])
            for i, (ref, buf) in enumerate(((w_hbm, w_buf), (m_hbm, m_buf), (g_hbm, g_buf)))
        ]

    def remote(src, dst, sem, k, **where):
        return pltpu.make_async_remote_copy(
            src, dst, sem.at[0, k], sem.at[1, k], device_id=where, device_id_type=MESH
        )

    def to_pair(k):
        return remote(pair_out.at[k], pair_in.at[k], pair_sem, k, dp=mate)

    def to_col(k):
        return remote(col.at[k], col_in.at[k], col_sem, k, dp=across)

    def to_fwd(k, up=4):
        return remote(fwd.at[k], fwd_in.at[k], fwd_sem, k, dp=at + up)

    def to_back(k, down=4):
        return remote(back.at[k], back_in.at[k], back_sem, k, dp=at - down)

    def to_mate(k):
        return remote(out_ref.at[k, share], out_ref.at[k, share], mate_sem, k, dp=mate)

    others = [lax.rem(group + step, groups) for step in range(1, groups)]

    def to_cross(k, i):
        return remote(
            out_ref.at[k, share], out_ref.at[k, share], cross_sem.at[i], k, groups=others[i]
        )

    def from_cross(k, i):
        sent_by = lax.rem(group + groups - 1 - i, groups)
        slot = 2 * sent_by + core
        return pltpu.make_async_remote_copy(
            out_ref.at[k, slot], out_ref.at[k, slot], cross_sem.at[i, 0, k], cross_sem.at[i, 1, k],
            device_id={"groups": others[i]}, device_id_type=MESH,
        )

    def to_pass(k, i):
        slot = 2 * lax.rem(group + groups - 1 - i, groups) + core
        return remote(out_ref.at[k, slot], out_ref.at[k, slot], pass_sem.at[i], k, dp=mate)

    def start_loads(k, carry):
        for copy in loads(k):
            copy.start()
        return carry

    lax.fori_loop(0, chunks, start_loads, 0)

    barrier = pltpu.get_barrier_semaphore()
    pl.semaphore_signal(barrier, inc=1, device_id={"dp": mate}, device_id_type=MESH)
    pl.semaphore_signal(barrier, inc=1, device_id={"dp": across}, device_id_type=MESH)
    for other in others:
        pl.semaphore_signal(barrier, inc=1, device_id={"groups": other}, device_id_type=MESH)

    @pl.when(z > 0)
    def _():
        pl.semaphore_signal(barrier, inc=1, device_id={"dp": at - 4}, device_id_type=MESH)

    @pl.when(z < last)
    def _():
        pl.semaphore_signal(barrier, inc=1, device_id={"dp": at + 4}, device_id_type=MESH)

    ahead, behind = jnp.where(z < last, 1, 0), jnp.where(z > 0, 1, 0)
    pl.semaphore_wait(barrier, 1 + groups + ahead + behind)

    def at_step(k, what):
        pl.when((k >= 0) & (k < chunks))(lambda: what(k))

    def renew(k):
        for copy in loads(k):
            copy.wait()
        mine = mask_ref[k] > 0.5

        def new(c):
            velocity = momentum_decay * m_buf[k, c] + g_buf[k, c].astype(jnp.float32)
            updated = w_buf[k, c].astype(jnp.float32) - learn_rate * velocity
            return jnp.where(mine, updated, 0.0).astype(jnp.bfloat16)

        pair_out[k] = new(1 - core)
        to_pair(k).start()
        own[k] = new(core)

    def join_pair(k):
        to_pair(k).wait_recv()
        col[k] = own[k] + pair_in[k]
        to_col(k).start()

    def join_col(k):
        to_col(k).wait_recv()
        joined[k] = col[k] + col_in[k]

    def go_fwd(k):
        @pl.when(z == 0)
        def _():
            fwd[k] = joined[k]

        @pl.when(z > 0)
        def _():
            to_fwd(k, -4).wait_recv()
            fwd[k] = joined[k] + fwd_in[k]

        @pl.when(z < last)
        def _():
            to_fwd(k).start()

    def go_back(k):
        @pl.when(z == last)
        def _():
            back[k] = joined[k]

        @pl.when(z < last)
        def _():
            to_back(k, -4).wait_recv()
            back[k] = joined[k] + back_in[k]

        @pl.when(z > 0)
        def _():
            to_back(k).start()

    def finish(k):
        @pl.when(z < last)
        def _():
            out_ref[k, share] = fwd[k] + back_in[k]

        @pl.when(z == last)
        def _():
            out_ref[k, share] = fwd[k]

        to_mate(k).start()
        for i in range(groups - 1):
            to_cross(k, i).start()

    def pass_on(k):
        for i in range(groups - 1):
            from_cross(k, i).wait_recv()
            to_pass(k, i).start()

    def step(t, carry):
        at_step(t, renew)
        at_step(t - 1, join_pair)
        begin = 1 + hop
        at_step(t - begin, join_col)
        at_step(t - begin - z * hop, go_fwd)
        at_step(t - begin - (last - z) * hop, go_back)
        at_step(t - begin - last * hop, finish)
        at_step(t - begin - last * hop - hop, pass_on)
        return carry

    lax.fori_loop(0, chunks + 1 + hop + last * hop + hop, step, 0)

    def drain(k, carry):
        to_pair(k).wait_send()
        to_col(k).wait_send()

        @pl.when(z < last)
        def _():
            to_fwd(k).wait_send()

        @pl.when(z > 0)
        def _():
            to_back(k).wait_send()

        to_mate(k).wait()
        for i in range(groups - 1):
            to_cross(k, i).wait_send()
            to_pass(k, i).wait()
        return carry

    lax.fori_loop(0, chunks, drain, 0)


def spread(kernel_weights, kernel_momentum, kernel_grads, owners):
    groups, dp = lax.axis_size("groups"), lax.axis_size("dp")
    _, kernels, rows, columns, fan_in, fan_out = kernel_weights.shape
    chunks, shares = kernels * rows * columns, 2 * groups
    part = fan_in // shares
    cut = lambda a: a.reshape(chunks, shares, part, fan_out)
    mine = (owners == lax.axis_index("dp")).astype(jnp.float32)
    mask = jnp.broadcast_to(
        jnp.repeat(mine, rows * columns)[:, None, None], (chunks, 1, fan_out)
    )
    piece = pltpu.VMEM((chunks, part, fan_out), jnp.bfloat16)
    load = lambda dtype: pltpu.VMEM((chunks, 2, part, fan_out), dtype)
    sems = pltpu.SemaphoreType.DMA((2, chunks))
    many = pltpu.SemaphoreType.DMA((groups - 1, 2, chunks))
    out = pl.pallas_call(
        functools.partial(spread_kernel, groups, dp // 4, chunks),
        out_shape=jax.ShapeDtypeStruct((chunks, shares, part, fan_out), jnp.bfloat16),
        in_specs=[pl.BlockSpec(memory_space=pltpu.VMEM)] + [pl.BlockSpec(memory_space=pl.ANY)] * 3,
        out_specs=pl.BlockSpec(memory_space=pltpu.VMEM),
        scratch_shapes=[load(jnp.bfloat16), load(jnp.float32), load(jnp.bfloat16)]
        + [piece] * 10
        + [pltpu.SemaphoreType.DMA((3, chunks)), sems, sems, sems, sems, sems, many, many],
        compiler_params=pltpu.CompilerParams(
            collective_id=0, has_side_effects=True, vmem_limit_bytes=56 << 20
        ),
    )(mask, cut(kernel_weights), cut(kernel_momentum), cut(kernel_grads))
    return out.reshape(kernels, rows * columns * fan_in, fan_out)


def silu(v):
    return v / (1.0 + jnp.exp(-v))


def conv_kernel(x_ref, top_ref, bottom_ref, k_ref, o_ref, patch, wide):
    height, channels, width = x_ref.shape[1:]

    @pl.when(pl.program_id(0) == 0)
    def _():
        wide[...] = k_ref[0].astype(jnp.float32).T.astype(jnp.bfloat16)

    conv_image(x_ref.at[0], top_ref.at[0, 0], bottom_ref.at[0, 0], o_ref.at[0], patch, wide)


def conv_image(x_ref, top_ref, bottom_ref, o_ref, patch, wide):
    height, channels, width = x_ref.shape
    column = lax.broadcasted_iota(jnp.int32, (1, width), 1)

    def build(row):
        if row == 0:
            v = top_ref[...]
        elif row == height + 1:
            v = bottom_ref[...]
        else:
            v = x_ref[row - 1]
        a = silu(v.astype(jnp.float32))
        before = jnp.where(column == 0, 0.0, pltpu.roll(a, 1, 1))
        after = jnp.where(column == width - 1, 0.0, pltpu.roll(a, width - 1, 1))
        for dc, part in enumerate((before, a, after)):
            patch[row, dc * channels : (dc + 1) * channels] = part.astype(jnp.bfloat16)

    built = 0
    for row in range(0, height, 2):
        while built < row + 4:
            build(built)
            built += 1
        rhs = jnp.concatenate(
            [
                jnp.concatenate([patch[row + dr], patch[row + dr + 1]], axis=1)
                for dr in range(3)
            ],
            axis=0,
        )
        acc = jnp.dot(wide[...], rhs, preferred_element_type=jnp.float32)
        for i in range(2):
            x = x_ref[row + i].astype(jnp.float32)
            o_ref[row + i] = (x + acc[:, i * width : (i + 1) * width]).astype(o_ref.dtype)


def residual_conv(x, kernels, which):
    images, height, channels, width = x.shape
    count = lax.axis_size("dp")
    top = lax.ppermute(x[:, -1:], "dp", [(i, i + 1) for i in range(count - 1)])
    bottom = lax.ppermute(x[:, :1], "dp", [(i + 1, i) for i in range(count - 1)])
    image = pl.BlockSpec((1, height, channels, width), lambda i: (i, 0, 0, 0))
    edge = pl.BlockSpec((1, 1, channels, width), lambda i: (i, 0, 0, 0))
    return pl.pallas_call(
        conv_kernel,
        out_shape=jax.ShapeDtypeStruct(x.shape, x.dtype),
        grid=(images,),
        in_specs=[image, edge, edge, pl.BlockSpec((1,) + kernels.shape[1:], lambda i: (which, 0, 0))],
        out_specs=image,
        scratch_shapes=[
            pltpu.VMEM((height + 2, 3 * channels, width), jnp.bfloat16),
            pltpu.VMEM(kernels.shape[:0:-1], jnp.bfloat16),
        ],
        compiler_params=pltpu.CompilerParams(vmem_limit_bytes=56 << 20),
    )(x, top, bottom, kernels)


def local(images, kernel_weights, kernel_momentum, kernel_grads, owners):
    kernels = spread(kernel_weights, kernel_momentum, kernel_grads, owners)
    hidden = residual_conv(images.transpose(0, 1, 3, 2), kernels, 0)
    return residual_conv(hidden, kernels, 1).transpose(0, 1, 3, 2)


def solution(mesh):
    placed = (
        P("groups", "dp", None, None),
        P("dp", None, None, None, None, None),
        P("dp", None, None, None, None, None),
        P("dp", None, None, None, None, None),
        P(),
    )
    return jax.shard_map(
        local, mesh=mesh, in_specs=placed, out_specs=P("groups", "dp", None, None), check_vma=False
    )
```

```python
import functools

import jax
import jax.numpy as jnp
from jax import lax
from jax.experimental import pallas as pl
from jax.experimental.pallas import tpu as pltpu
from jax.sharding import PartitionSpec as P

momentum_decay = 0.9
learn_rate = 0.5
MESH = pl.DeviceIdType.MESH
fine_chunks = 15
coarse_chunks = 3
pair_hop = 3
hop = 4


class Place:
    def __init__(self, groups, dp):
        self.groups, self.dp, self.last = groups, dp, dp // 4 - 1
        self.group, self.at = lax.axis_index("groups"), lax.axis_index("dp")
        self.z, self.y, self.core = self.at // 4, (self.at // 2) % 2, self.at % 2
        self.mate = self.at + 1 - 2 * self.core
        self.beside = self.at - 1 + 2 * self.core
        self.across = self.at + 2 - 4 * self.y
        self.share = 2 * self.group + self.core
        self.others = [lax.rem(self.group + step, groups) for step in range(1, groups)]
        self.has_beside = (self.beside >= 0) & (self.beside < dp)

    def meet(self):
        barrier = pltpu.get_barrier_semaphore()

        def greet(**where):
            pl.semaphore_signal(barrier, inc=1, device_id=where, device_id_type=MESH)

        greet(dp=self.mate)
        greet(dp=self.across)
        for other in self.others:
            greet(groups=other)
        pl.when(self.has_beside)(lambda: greet(dp=self.beside))
        pl.when(self.z > 0)(lambda: greet(dp=self.at - 4))
        pl.when(self.z < self.last)(lambda: greet(dp=self.at + 4))
        more = [
            jnp.where(there, 1, 0)
            for there in (self.has_beside, self.z > 0, self.z < self.last)
        ]
        pl.semaphore_wait(barrier, 1 + self.groups + sum(more))


def remote(src, dst, sem, k, **where):
    return pltpu.make_async_remote_copy(
        src, dst, sem.at[0, k], sem.at[1, k], device_id=where, device_id_type=MESH
    )


class Stream:
    def __init__(self, place, col, out, col_in, joined, fwd, fwd_in, back, back_in, done, sems):
        self.__dict__.update(place=place, col=col, out=out, col_in=col_in, joined=joined)
        self.__dict__.update(fwd=fwd, fwd_in=fwd_in, back=back, back_in=back_in, done=done)
        self.col_sem, self.fwd_sem, self.back_sem, self.mate_sem = sems[:4]
        self.cross_sem, self.pass_sem, self.keep_sem = sems[4:]

    def to_col(self, k):
        return remote(self.col.at[k], self.col_in.at[k], self.col_sem, k, dp=self.place.across)

    def to_fwd(self, k, up=4):
        return remote(self.fwd.at[k], self.fwd_in.at[k], self.fwd_sem, k, dp=self.place.at + up)

    def to_back(self, k, down=4):
        return remote(self.back.at[k], self.back_in.at[k], self.back_sem, k, dp=self.place.at - down)

    def keep(self, k):
        return pltpu.make_async_copy(
            self.done.at[k], self.out.at[k, self.place.share], self.keep_sem.at[k]
        )

    def to_mate(self, k):
        return remote(
            self.done.at[k], self.out.at[k, self.place.share], self.mate_sem, k, dp=self.place.mate
        )

    def to_cross(self, k, i):
        return remote(
            self.done.at[k], self.out.at[k, self.place.share], self.cross_sem.at[i], k,
            groups=self.place.others[i],
        )

    def to_pass(self, k, i):
        p = self.place
        slot = 2 * lax.rem(p.group + p.groups - 1 - i, p.groups) + p.core
        return remote(self.out.at[k, slot], self.out.at[k, slot], self.pass_sem.at[i], k, dp=p.mate)

    def join_col(self, k):
        self.to_col(k).wait_recv()
        self.joined[k] = self.col[k] + self.col_in[k]

    def go_fwd(self, k):
        p = self.place

        @pl.when(p.z == 0)
        def _():
            self.fwd[k] = self.joined[k]

        @pl.when(p.z > 0)
        def _():
            self.to_fwd(k, -4).wait_recv()
            self.fwd[k] = self.joined[k] + self.fwd_in[k]

        pl.when(p.z < p.last)(lambda: self.to_fwd(k).start())

    def go_back(self, k):
        p = self.place

        @pl.when(p.z == p.last)
        def _():
            self.back[k] = self.joined[k]

        @pl.when(p.z < p.last)
        def _():
            self.to_back(k, -4).wait_recv()
            self.back[k] = self.joined[k] + self.back_in[k]

        pl.when(p.z > 0)(lambda: self.to_back(k).start())

    def finish(self, k):
        p = self.place

        @pl.when(p.z < p.last)
        def _():
            self.done[k] = self.fwd[k] + self.back_in[k]

        @pl.when(p.z == p.last)
        def _():
            self.done[k] = self.fwd[k]

        for i in range(p.groups - 1):
            self.to_cross(k, i).start()
        self.to_mate(k).start()
        self.keep(k).start()

    def pass_on(self, k):
        for i in range(self.place.groups - 1):
            self.to_cross(k, i).wait_recv()
            self.to_pass(k, i).start()

    def steps(self, chunks, hop):
        return chunks + hop * (self.place.last + 2)

    def step(self, t, chunks, hop):
        p = self.place
        at_step(t - hop, chunks, self.join_col)
        at_step(t - hop - p.z * hop, chunks, self.go_fwd)
        at_step(t - hop - (p.last - p.z) * hop, chunks, self.go_back)
        at_step(t - hop - p.last * hop, chunks, self.finish)
        at_step(t - hop - p.last * hop - hop, chunks, self.pass_on)

    def drain(self, k):
        p = self.place
        self.to_col(k).wait_send()
        pl.when(p.z < p.last)(lambda: self.to_fwd(k).wait_send())
        pl.when(p.z > 0)(lambda: self.to_back(k).wait_send())
        self.to_mate(k).wait()
        self.keep(k).wait()
        for i in range(p.groups - 1):
            self.to_cross(k, i).wait_send()
            self.to_pass(k, i).wait()

    @staticmethod
    def scratch(chunks, part, width, groups):
        piece = pltpu.VMEM((chunks, part, width), jnp.bfloat16)
        sems = pltpu.SemaphoreType.DMA((2, chunks))
        many = pltpu.SemaphoreType.DMA((groups - 1, 2, chunks))
        return [piece] * 7 + [sems] * 4 + [many] * 2 + [pltpu.SemaphoreType.DMA((chunks,))]


def at_step(k, chunks, what):
    pl.when((k >= 0) & (k < chunks))(lambda: what(k))


def each(chunks, what):
    def body(k, carry):
        what(k)
        return carry

    lax.fori_loop(0, chunks, body, 0)


class Edges:
    def __init__(self, place, first, final, out, sem):
        self.place, self.first, self.final, self.out, self.sem = place, first, final, out, sem

    def down(self, k, to=1):
        return remote(self.final(k), self.out(0, k), self.sem.at[0], k, dp=self.place.at + to)

    def up(self, k, to=1):
        return remote(self.first(k), self.out(1, k), self.sem.at[1], k, dp=self.place.at - to)

    def start(self, k):
        at, dp = self.place.at, self.place.dp
        pl.when(at < dp - 1)(lambda: self.down(k).start())
        pl.when(at > 0)(lambda: self.up(k).start())

    def drain(self, k):
        at, dp = self.place.at, self.place.dp

        @pl.when(at < dp - 1)
        def _():
            self.down(k).wait_send()
            self.up(k, -1).wait_recv()

        @pl.when(at > 0)
        def _():
            self.up(k).wait_send()
            self.down(k, -1).wait_recv()


class Renewal:
    def __init__(self, place, mask, base, state, bufs, col, pair_out, pair_in, load_sem, pair_sem):
        self.place, self.mask, self.base = place, mask, base
        self.state, self.bufs = state, bufs
        self.col, self.pair_out, self.pair_in = col, pair_out, pair_in
        self.load_sem, self.pair_sem = load_sem, pair_sem

    def loads(self, k):
        src = pl.ds(2 * self.place.group, 2)
        return [
            pltpu.make_async_copy(ref.at[self.base + k, src], buf.at[k], self.load_sem.at[i, k])
            for i, (ref, buf) in enumerate(zip(self.state, self.bufs))
        ]

    def start(self, k):
        for copy in self.loads(k):
            copy.start()

    def to_pair(self, k):
        return remote(
            self.pair_out.at[k], self.pair_in.at[k], self.pair_sem, k, dp=self.place.mate
        )

    def renew(self, k):
        for copy in self.loads(k):
            copy.wait()
        w, m, g = self.bufs
        mine = self.mask > 0.5

        def new(c):
            velocity = momentum_decay * m[k, c] + g[k, c].astype(jnp.float32)
            updated = w[k, c].astype(jnp.float32) - learn_rate * velocity
            return jnp.where(mine, updated, 0.0).astype(jnp.bfloat16)

        self.pair_out[k] = new(1 - self.place.core)
        self.to_pair(k).start()
        self.col[k] = new(self.place.core)

    def join(self, k):
        self.to_pair(k).wait_recv()
        self.col[k] = self.col[k] + self.pair_in[k]

    @staticmethod
    def scratch(chunks, part, width):
        load = lambda dtype: pltpu.VMEM((chunks, 2, part, width), dtype)
        piece = pltpu.VMEM((chunks, part, width), jnp.bfloat16)
        return [load(jnp.bfloat16), load(jnp.float32), load(jnp.bfloat16), piece, piece] + [
            pltpu.SemaphoreType.DMA((3, chunks)),
            pltpu.SemaphoreType.DMA((2, chunks)),
        ]


def spread_kernel(groups, dp, mask_ref, *refs):
    first_state, second_state, x_ref, out_ref, col1_ref, rims_ref = (
        refs[:3], refs[3:6], refs[6], refs[7], refs[8], refs[9],
    )
    scratch = refs[10:]
    place = Place(groups, dp)
    one = Renewal(place, mask_ref[0], 0, first_state, scratch[:3], scratch[14], *scratch[3:7])
    two = Renewal(place, mask_ref[1], coarse_chunks, second_state, scratch[7:10], col1_ref, *scratch[10:14])
    stream = Stream(place, scratch[14], out_ref, *scratch[15:22], scratch[22:29])
    height = x_ref.shape[1]
    edges = Edges(
        place, lambda k: x_ref.at[:, 0], lambda k: x_ref.at[:, height - 1],
        lambda side, k: rims_ref.at[side], scratch[29],
    )
    each(fine_chunks, one.start)
    each(coarse_chunks, two.start)
    place.meet()

    def join(k):
        one.join(k)
        stream.to_col(k).start()

    def step(t, carry):
        at_step(t, fine_chunks, one.renew)
        at_step(t - pair_hop, fine_chunks, join)
        stream.step(t - pair_hop, fine_chunks, hop)
        late = t - fine_chunks - pair_hop
        pl.when(late == 0)(lambda: edges.start(0))
        at_step(late - 1, coarse_chunks, two.renew)
        at_step(late - 1 - pair_hop, coarse_chunks, two.join)
        return carry

    lax.fori_loop(0, pair_hop + stream.steps(fine_chunks, hop), step, 0)

    def drain(k):
        one.to_pair(k).wait_send()
        stream.drain(k)

    each(fine_chunks, drain)
    each(coarse_chunks, lambda k: two.to_pair(k).wait_send())
    edges.drain(0)


def spread(kernel_weights, kernel_momentum, kernel_grads, owners, x):
    groups, dp = lax.axis_size("groups"), lax.axis_size("dp")
    _, _, rows, columns, fan_in, fan_out = kernel_weights.shape
    images, _, channels, width = x.shape
    shares, depth = 2 * groups, rows * columns * fan_in
    mine = (owners == lax.axis_index("dp")).astype(jnp.float32)
    mask = jnp.broadcast_to(mine[:, None, None], (2, 1, fan_out))
    state = (kernel_weights, kernel_momentum, kernel_grads)

    def cut(chunks):
        return [a.reshape(2 * chunks, shares, -1, fan_out) for a in state]

    fine, coarse = depth // fine_chunks // shares, depth // coarse_chunks // shares
    any_space = pl.BlockSpec(memory_space=pl.ANY)
    vmem = pl.BlockSpec(memory_space=pltpu.VMEM)
    kernel, col, rims = pl.pallas_call(
        functools.partial(spread_kernel, groups, dp),
        out_shape=[
            jax.ShapeDtypeStruct((fine_chunks, shares, fine, fan_out), jnp.bfloat16),
            jax.ShapeDtypeStruct((coarse_chunks, coarse, fan_out), jnp.bfloat16),
            jax.ShapeDtypeStruct((2, images, channels, width), jnp.bfloat16),
        ],
        in_specs=[vmem] + [any_space] * 7,
        out_specs=[vmem, vmem, any_space],
        scratch_shapes=Renewal.scratch(fine_chunks, fine, fan_out)
        + Renewal.scratch(coarse_chunks, coarse, fan_out)
        + [pltpu.VMEM((fine_chunks, fine, fan_out), jnp.bfloat16)]
        + Stream.scratch(fine_chunks, fine, fan_out, groups)
        + [pltpu.SemaphoreType.DMA((2, 2, 1))],
        compiler_params=pltpu.CompilerParams(
            collective_id=0, has_side_effects=True, vmem_limit_bytes=56 << 20
        ),
    )(mask, *cut(fine_chunks), *cut(coarse_chunks), x)
    return kernel.reshape(depth, fan_out), col, rims


def silu(v):
    return v / (1.0 + jnp.exp(-v))


def conv_image(x_ref, top_ref, bottom_ref, o_ref, patch, wide):
    height, channels, width = x_ref.shape
    at = lax.axis_index("dp")
    column = lax.broadcasted_iota(jnp.int32, (1, width), 1)

    def build(row):
        if row == 0:
            v = jnp.where(at > 0, top_ref[...].astype(jnp.float32), 0.0)
        elif row == height + 1:
            v = jnp.where(at < lax.axis_size("dp") - 1, bottom_ref[...].astype(jnp.float32), 0.0)
        else:
            v = x_ref[row - 1]
        a = silu(v.astype(jnp.float32))
        before = jnp.where(column == 0, 0.0, pltpu.roll(a, 1, 1))
        after = jnp.where(column == width - 1, 0.0, pltpu.roll(a, width - 1, 1))
        for dc, part in enumerate((before, a, after)):
            patch[row, dc * channels : (dc + 1) * channels] = part.astype(jnp.bfloat16)

    built = 0
    for row in range(0, height, 2):
        while built < row + 4:
            build(built)
            built += 1
        rhs = jnp.concatenate(
            [
                jnp.concatenate([patch[row + dr], patch[row + dr + 1]], axis=1)
                for dr in range(3)
            ],
            axis=0,
        )
        acc = jnp.dot(wide[...], rhs, preferred_element_type=jnp.float32)
        for i in range(2):
            x = x_ref[row + i].astype(jnp.float32)
            o_ref[row + i] = (x + acc[:, i * width : (i + 1) * width]).astype(o_ref.dtype)


def first_kernel(groups, dp, x_ref, top_ref, bottom_ref, k_ref, col_ref, o_ref, out_ref, rims_ref,
                 patch, wide, borders, edge_sem, *scratch):
    place = Place(groups, dp)
    image, images = pl.program_id(0), pl.num_programs(0)
    height = x_ref.shape[1]
    stream = Stream(place, col_ref, out_ref, *scratch[:7], scratch[7:])
    edges = Edges(
        place, lambda k: borders.at[k, 0], lambda k: borders.at[k, 1],
        lambda side, k: rims_ref.at[side, k], edge_sem,
    )

    @pl.when(image == 0)
    def _():
        place.meet()
        wide[...] = k_ref[...].astype(jnp.float32).T.astype(jnp.bfloat16)

    def step(t, carry=0):
        at_step(t, coarse_chunks, lambda k: stream.to_col(k).start())
        stream.step(t, coarse_chunks, 1)
        return carry

    step(image)
    conv_image(x_ref.at[0], top_ref.at[0, 0], bottom_ref.at[0, 0], o_ref.at[0], patch, wide)
    borders[image, 0] = o_ref[0, 0]
    borders[image, 1] = o_ref[0, height - 1]
    edges.start(image)

    @pl.when(image == images - 1)
    def _():
        count = borders.shape[0]
        lax.fori_loop(count, max(count, stream.steps(coarse_chunks, 1)), step, 0)
        each(coarse_chunks, stream.drain)
        each(count, edges.drain)


def second_kernel(x_ref, top_ref, bottom_ref, k_ref, o_ref, patch, wide):
    @pl.when(pl.program_id(0) == 0)
    def _():
        wide[...] = k_ref[...].astype(jnp.float32).T.astype(jnp.bfloat16)

    conv_image(x_ref.at[0], top_ref.at[0, 0], bottom_ref.at[0, 0], o_ref.at[0], patch, wide)


def conv_specs(x, kernel):
    images, height, channels, width = x.shape
    image = pl.BlockSpec((1, height, channels, width), lambda i: (i, 0, 0, 0))
    top = pl.BlockSpec((1, 1, channels, width), lambda i: (0, i, 0, 0))
    bottom = pl.BlockSpec((1, 1, channels, width), lambda i: (1, i, 0, 0))
    scratch = [
        pltpu.VMEM((height + 2, 3 * channels, width), jnp.bfloat16),
        pltpu.VMEM(kernel.shape[::-1], jnp.bfloat16),
    ]
    return image, [image, top, bottom, pl.BlockSpec(kernel.shape, lambda i: (0, 0))], scratch


def first_conv(x, rims, kernel, col):
    groups, dp = lax.axis_size("groups"), lax.axis_size("dp")
    images, height, channels, width = x.shape
    chunks, part, fan_out = col.shape
    image, in_specs, scratch = conv_specs(x, kernel)
    any_space = pl.BlockSpec(memory_space=pl.ANY)
    hidden, second, rims = pl.pallas_call(
        functools.partial(first_kernel, groups, dp),
        out_shape=[
            jax.ShapeDtypeStruct(x.shape, x.dtype),
            jax.ShapeDtypeStruct((chunks, 2 * groups, part, fan_out), jnp.bfloat16),
            jax.ShapeDtypeStruct(rims.shape, rims.dtype),
        ],
        grid=(images,),
        in_specs=in_specs + [pl.BlockSpec(col.shape, lambda i: (0, 0, 0))],
        out_specs=[image, any_space, any_space],
        scratch_shapes=scratch
        + [
            pltpu.VMEM((images, 2, channels, width), jnp.bfloat16),
            pltpu.SemaphoreType.DMA((2, 2, images)),
        ]
        + Stream.scratch(chunks, part, fan_out, groups),
        compiler_params=pltpu.CompilerParams(
            collective_id=1, has_side_effects=True, vmem_limit_bytes=56 << 20
        ),
    )(x, rims, rims, kernel, col)
    return hidden, second.reshape(kernel.shape), rims


def second_conv(x, rims, kernel):
    image, in_specs, scratch = conv_specs(x, kernel)
    return pl.pallas_call(
        second_kernel,
        out_shape=jax.ShapeDtypeStruct(x.shape, x.dtype),
        grid=(x.shape[0],),
        in_specs=in_specs,
        out_specs=image,
        scratch_shapes=scratch,
        compiler_params=pltpu.CompilerParams(vmem_limit_bytes=56 << 20),
    )(x, rims, rims, kernel)


def local(images, kernel_weights, kernel_momentum, kernel_grads, owners):
    x = images.transpose(0, 1, 3, 2)
    kernel, col, rims = spread(kernel_weights, kernel_momentum, kernel_grads, owners, x)
    hidden, kernel, rims = first_conv(x, rims, kernel, col)
    return second_conv(hidden, rims, kernel).transpose(0, 1, 3, 2)


def solution(mesh):
    placed = (
        P("groups", "dp", None, None),
        P("dp", None, None, None, None, None),
        P("dp", None, None, None, None, None),
        P("dp", None, None, None, None, None),
        P(),
    )
    return jax.shard_map(
        local, mesh=mesh, in_specs=placed, out_specs=P("groups", "dp", None, None), check_vma=False
    )
```

```python
import functools

import jax
import jax.numpy as jnp
from jax import lax
from jax.experimental import pallas as pl
from jax.experimental.pallas import tpu as pltpu
from jax.sharding import PartitionSpec as P

momentum_decay = 0.9
learn_rate = 0.5
MESH = pl.DeviceIdType.MESH
fine_chunks = 15
coarse_chunks = 3
pair_hop = 3
hop = 4


class Place:
    def __init__(self, groups, dp):
        self.groups, self.dp, self.last = groups, dp, dp // 4 - 1
        self.group, self.at = lax.axis_index("groups"), lax.axis_index("dp")
        self.z, self.y, self.core = self.at // 4, (self.at // 2) % 2, self.at % 2
        self.mate = self.at + 1 - 2 * self.core
        self.beside = self.at - 1 + 2 * self.core
        self.across = self.at + 2 - 4 * self.y
        self.share = 2 * self.group + self.core
        self.others = [lax.rem(self.group + step, groups) for step in range(1, groups)]
        self.has_beside = (self.beside >= 0) & (self.beside < dp)

    def meet(self):
        barrier = pltpu.get_barrier_semaphore()

        def greet(**where):
            pl.semaphore_signal(barrier, inc=1, device_id=where, device_id_type=MESH)

        greet(dp=self.mate)
        greet(dp=self.across)
        for other in self.others:
            greet(groups=other)
        pl.when(self.has_beside)(lambda: greet(dp=self.beside))
        pl.when(self.z > 0)(lambda: greet(dp=self.at - 4))
        pl.when(self.z < self.last)(lambda: greet(dp=self.at + 4))
        more = [
            jnp.where(there, 1, 0)
            for there in (self.has_beside, self.z > 0, self.z < self.last)
        ]
        pl.semaphore_wait(barrier, 1 + self.groups + sum(more))


def remote(src, dst, sem, k, **where):
    return pltpu.make_async_remote_copy(
        src, dst, sem.at[0, k], sem.at[1, k], device_id=where, device_id_type=MESH
    )


class Stream:
    def __init__(self, place, col, out, col_in, joined, fwd, fwd_in, back, back_in, done, sems):
        self.__dict__.update(place=place, col=col, out=out, col_in=col_in, joined=joined)
        self.__dict__.update(fwd=fwd, fwd_in=fwd_in, back=back, back_in=back_in, done=done)
        self.col_sem, self.fwd_sem, self.back_sem, self.mate_sem = sems[:4]
        self.cross_sem, self.pass_sem, self.keep_sem = sems[4:]

    def to_col(self, k):
        return remote(self.col.at[k], self.col_in.at[k], self.col_sem, k, dp=self.place.across)

    def to_fwd(self, k, up=4):
        return remote(self.fwd.at[k], self.fwd_in.at[k], self.fwd_sem, k, dp=self.place.at + up)

    def to_back(self, k, down=4):
        return remote(self.back.at[k], self.back_in.at[k], self.back_sem, k, dp=self.place.at - down)

    def keep(self, k):
        return pltpu.make_async_copy(
            self.done.at[k], self.out.at[k, self.place.share], self.keep_sem.at[k]
        )

    def to_mate(self, k):
        return remote(
            self.done.at[k], self.out.at[k, self.place.share], self.mate_sem, k, dp=self.place.mate
        )

    def to_cross(self, k, i):
        return remote(
            self.done.at[k], self.out.at[k, self.place.share], self.cross_sem.at[i], k,
            groups=self.place.others[i],
        )

    def to_pass(self, k, i):
        p = self.place
        slot = 2 * lax.rem(p.group + p.groups - 1 - i, p.groups) + p.core
        return remote(self.out.at[k, slot], self.out.at[k, slot], self.pass_sem.at[i], k, dp=p.mate)

    def join_col(self, k):
        self.to_col(k).wait_recv()
        self.joined[k] = self.col[k] + self.col_in[k]

    def go_fwd(self, k):
        p = self.place

        @pl.when(p.z == 0)
        def _():
            self.fwd[k] = self.joined[k]

        @pl.when(p.z > 0)
        def _():
            self.to_fwd(k, -4).wait_recv()
            self.fwd[k] = self.joined[k] + self.fwd_in[k]

        pl.when(p.z < p.last)(lambda: self.to_fwd(k).start())

    def go_back(self, k):
        p = self.place

        @pl.when(p.z == p.last)
        def _():
            self.back[k] = self.joined[k]

        @pl.when(p.z < p.last)
        def _():
            self.to_back(k, -4).wait_recv()
            self.back[k] = self.joined[k] + self.back_in[k]

        pl.when(p.z > 0)(lambda: self.to_back(k).start())

    def finish(self, k):
        p = self.place

        @pl.when(p.z < p.last)
        def _():
            self.done[k] = self.fwd[k] + self.back_in[k]

        @pl.when(p.z == p.last)
        def _():
            self.done[k] = self.fwd[k]

        for i in range(p.groups - 1):
            self.to_cross(k, i).start()
        self.to_mate(k).start()
        self.keep(k).start()

    def pass_on(self, k):
        for i in range(self.place.groups - 1):
            self.to_cross(k, i).wait_recv()
            self.to_pass(k, i).start()

    def steps(self, chunks, hop):
        return chunks + hop * (self.place.last + 2)

    def step(self, t, chunks, hop):
        p = self.place
        at_step(t - hop, chunks, self.join_col)
        at_step(t - hop - p.z * hop, chunks, self.go_fwd)
        at_step(t - hop - (p.last - p.z) * hop, chunks, self.go_back)
        at_step(t - hop - p.last * hop, chunks, self.finish)
        at_step(t - hop - p.last * hop - hop, chunks, self.pass_on)

    def drain(self, k):
        p = self.place
        self.to_col(k).wait_send()
        pl.when(p.z < p.last)(lambda: self.to_fwd(k).wait_send())
        pl.when(p.z > 0)(lambda: self.to_back(k).wait_send())
        self.to_mate(k).wait()
        self.keep(k).wait()
        for i in range(p.groups - 1):
            self.to_cross(k, i).wait_send()
            self.to_pass(k, i).wait()

    @staticmethod
    def scratch(chunks, part, width, groups):
        piece = pltpu.VMEM((chunks, part, width), jnp.bfloat16)
        sems = pltpu.SemaphoreType.DMA((2, chunks))
        many = pltpu.SemaphoreType.DMA((groups - 1, 2, chunks))
        return [piece] * 7 + [sems] * 4 + [many] * 2 + [pltpu.SemaphoreType.DMA((chunks,))]


def half_rows(part):
    return -(-(part // 2) // 8) * 8


def packed_rows(part, width):
    return width // 128 * part + (half_rows(part) if width % 128 else 0)


def packed(v):
    part, width = v.shape
    full, half = width // 128 * 128, half_rows(part)
    blocks = [v[:, i : i + 128] for i in range(0, full, 128)]
    if full < width:
        low, high = v[:half, full:], v[half:, full:]
        if part < 2 * half:
            high = jnp.concatenate(
                [high, jnp.zeros((2 * half - part, width - full), v.dtype)], axis=0
            )
        blocks.append(jnp.concatenate([low, high], axis=1))
    return jnp.concatenate(blocks, axis=0)


def unpack(k_ref, natural):
    chunks, shares, _, _ = k_ref.shape
    depth, width = natural.shape
    part = depth // (chunks * shares)
    full, half = width // 128 * 128, half_rows(part)
    for piece in range(chunks * shares):
        v = k_ref[piece // shares, piece % shares].astype(jnp.float32)
        base = piece * part
        for i in range(full // 128):
            natural[base : base + part, i * 128 : (i + 1) * 128] = v[i * part : (i + 1) * part]
        if full < width:
            rest = v[full // 128 * part :]
            natural[base : base + half, full:] = rest[:, : width - full]
            natural[base + half : base + part, full:] = rest[: part - half, width - full :]


def at_step(k, chunks, what):
    pl.when((k >= 0) & (k < chunks))(lambda: what(k))


def each(chunks, what):
    def body(k, carry):
        what(k)
        return carry

    lax.fori_loop(0, chunks, body, 0)


class Edges:
    def __init__(self, place, first, final, out, sem):
        self.place, self.first, self.final, self.out, self.sem = place, first, final, out, sem

    def down(self, k, to=1):
        return remote(self.final(k), self.out(0, k), self.sem.at[0], k, dp=self.place.at + to)

    def up(self, k, to=1):
        return remote(self.first(k), self.out(1, k), self.sem.at[1], k, dp=self.place.at - to)

    def start(self, k):
        at, dp = self.place.at, self.place.dp
        pl.when(at < dp - 1)(lambda: self.down(k).start())
        pl.when(at > 0)(lambda: self.up(k).start())

    def drain(self, k):
        at, dp = self.place.at, self.place.dp

        @pl.when(at < dp - 1)
        def _():
            self.down(k).wait_send()
            self.up(k, -1).wait_recv()

        @pl.when(at > 0)
        def _():
            self.up(k).wait_send()
            self.down(k, -1).wait_recv()


class Renewal:
    def __init__(self, place, mask, base, state, bufs, col, pair_out, pair_in, load_sem, pair_sem):
        self.place, self.mask, self.base = place, mask, base
        self.state, self.bufs = state, bufs
        self.col, self.pair_out, self.pair_in = col, pair_out, pair_in
        self.load_sem, self.pair_sem = load_sem, pair_sem

    def loads(self, k):
        src = pl.ds(2 * self.place.group, 2)
        return [
            pltpu.make_async_copy(ref.at[self.base + k, src], buf.at[k], self.load_sem.at[i, k])
            for i, (ref, buf) in enumerate(zip(self.state, self.bufs))
        ]

    def start(self, k):
        for copy in self.loads(k):
            copy.start()

    def to_pair(self, k):
        return remote(
            self.pair_out.at[k], self.pair_in.at[k], self.pair_sem, k, dp=self.place.mate
        )

    def renew(self, k):
        for copy in self.loads(k):
            copy.wait()
        w, m, g = self.bufs
        mine = self.mask > 0.5

        def new(c):
            velocity = momentum_decay * m[k, c] + g[k, c].astype(jnp.float32)
            updated = w[k, c].astype(jnp.float32) - learn_rate * velocity
            return packed(jnp.where(mine, updated, 0.0)).astype(jnp.bfloat16)

        self.pair_out[k] = new(1 - self.place.core)
        self.to_pair(k).start()
        self.col[k] = new(self.place.core)

    def join(self, k):
        self.to_pair(k).wait_recv()
        self.col[k] = self.col[k] + self.pair_in[k]

    @staticmethod
    def scratch(chunks, part, width):
        load = lambda dtype: pltpu.VMEM((chunks, 2, part, width), dtype)
        piece = pltpu.VMEM((chunks, packed_rows(part, width), 128), jnp.bfloat16)
        return [load(jnp.bfloat16), load(jnp.float32), load(jnp.bfloat16), piece, piece] + [
            pltpu.SemaphoreType.DMA((3, chunks)),
            pltpu.SemaphoreType.DMA((2, chunks)),
        ]


def spread_kernel(groups, dp, mask_ref, *refs):
    first_state, second_state, x_ref, out_ref, col1_ref, rims_ref = (
        refs[:3], refs[3:6], refs[6], refs[7], refs[8], refs[9],
    )
    scratch = refs[10:]
    place = Place(groups, dp)
    one = Renewal(place, mask_ref[0], 0, first_state, scratch[:3], scratch[14], *scratch[3:7])
    two = Renewal(place, mask_ref[1], coarse_chunks, second_state, scratch[7:10], col1_ref, *scratch[10:14])
    stream = Stream(place, scratch[14], out_ref, *scratch[15:22], scratch[22:29])
    height = x_ref.shape[1]
    edges = Edges(
        place, lambda k: x_ref.at[:, 0], lambda k: x_ref.at[:, height - 1],
        lambda side, k: rims_ref.at[side], scratch[29],
    )
    each(fine_chunks, one.start)
    each(coarse_chunks, two.start)
    place.meet()

    def join(k):
        one.join(k)
        stream.to_col(k).start()

    def step(t, carry):
        at_step(t, fine_chunks, one.renew)
        at_step(t - pair_hop, fine_chunks, join)
        stream.step(t - pair_hop, fine_chunks, hop)
        late = t - fine_chunks - pair_hop
        pl.when(late == 0)(lambda: edges.start(0))
        at_step(late - 1, coarse_chunks, two.renew)
        at_step(late - 1 - pair_hop, coarse_chunks, two.join)
        return carry

    lax.fori_loop(0, pair_hop + stream.steps(fine_chunks, hop), step, 0)

    def drain(k):
        one.to_pair(k).wait_send()
        stream.drain(k)

    each(fine_chunks, drain)
    each(coarse_chunks, lambda k: two.to_pair(k).wait_send())
    edges.drain(0)


def spread(kernel_weights, kernel_momentum, kernel_grads, owners, x):
    groups, dp = lax.axis_size("groups"), lax.axis_size("dp")
    _, _, rows, columns, fan_in, fan_out = kernel_weights.shape
    images, _, channels, width = x.shape
    shares, depth = 2 * groups, rows * columns * fan_in
    mine = (owners == lax.axis_index("dp")).astype(jnp.float32)
    mask = jnp.broadcast_to(mine[:, None, None], (2, 1, fan_out))
    state = (kernel_weights, kernel_momentum, kernel_grads)

    def cut(chunks):
        return [a.reshape(2 * chunks, shares, -1, fan_out) for a in state]

    fine, coarse = depth // fine_chunks // shares, depth // coarse_chunks // shares
    fine_rows, coarse_rows = packed_rows(fine, fan_out), packed_rows(coarse, fan_out)
    any_space = pl.BlockSpec(memory_space=pl.ANY)
    vmem = pl.BlockSpec(memory_space=pltpu.VMEM)
    kernel, col, rims = pl.pallas_call(
        functools.partial(spread_kernel, groups, dp),
        out_shape=[
            jax.ShapeDtypeStruct((fine_chunks, shares, fine_rows, 128), jnp.bfloat16),
            jax.ShapeDtypeStruct((coarse_chunks, coarse_rows, 128), jnp.bfloat16),
            jax.ShapeDtypeStruct((2, images, channels, width), jnp.bfloat16),
        ],
        in_specs=[vmem] + [any_space] * 7,
        out_specs=[vmem, vmem, any_space],
        scratch_shapes=Renewal.scratch(fine_chunks, fine, fan_out)
        + Renewal.scratch(coarse_chunks, coarse, fan_out)
        + [pltpu.VMEM((fine_chunks, fine_rows, 128), jnp.bfloat16)]
        + Stream.scratch(fine_chunks, fine_rows, 128, groups)
        + [pltpu.SemaphoreType.DMA((2, 2, 1))],
        compiler_params=pltpu.CompilerParams(
            collective_id=0, has_side_effects=True, vmem_limit_bytes=56 << 20
        ),
    )(mask, *cut(fine_chunks), *cut(coarse_chunks), x)
    return kernel, col, rims


def silu(v):
    return v / (1.0 + jnp.exp(-v))


def conv_image(x_ref, top_ref, bottom_ref, o_ref, patch, wide):
    height, channels, width = x_ref.shape
    at = lax.axis_index("dp")
    column = lax.broadcasted_iota(jnp.int32, (1, width), 1)

    def build(row):
        if row == 0:
            v = jnp.where(at > 0, top_ref[...].astype(jnp.float32), 0.0)
        elif row == height + 1:
            v = jnp.where(at < lax.axis_size("dp") - 1, bottom_ref[...].astype(jnp.float32), 0.0)
        else:
            v = x_ref[row - 1]
        a = silu(v.astype(jnp.float32))
        before = jnp.where(column == 0, 0.0, pltpu.roll(a, 1, 1))
        after = jnp.where(column == width - 1, 0.0, pltpu.roll(a, width - 1, 1))
        for dc, part in enumerate((before, a, after)):
            patch[row, dc * channels : (dc + 1) * channels] = part.astype(jnp.bfloat16)

    built = 0
    for row in range(0, height, 2):
        while built < row + 4:
            build(built)
            built += 1
        rhs = jnp.concatenate(
            [
                jnp.concatenate([patch[row + dr], patch[row + dr + 1]], axis=1)
                for dr in range(3)
            ],
            axis=0,
        )
        acc = jnp.dot(wide[...], rhs, preferred_element_type=jnp.float32)
        for i in range(2):
            x = x_ref[row + i].astype(jnp.float32)
            o_ref[row + i] = (x + acc[:, i * width : (i + 1) * width]).astype(o_ref.dtype)


def first_kernel(groups, dp, x_ref, top_ref, bottom_ref, k_ref, col_ref, o_ref, out_ref, rims_ref,
                 patch, wide, natural, borders, edge_sem, *scratch):
    place = Place(groups, dp)
    image, images = pl.program_id(0), pl.num_programs(0)
    height = x_ref.shape[1]
    stream = Stream(place, col_ref, out_ref, *scratch[:7], scratch[7:])
    edges = Edges(
        place, lambda k: borders.at[k, 0], lambda k: borders.at[k, 1],
        lambda side, k: rims_ref.at[side, k], edge_sem,
    )

    @pl.when(image == 0)
    def _():
        place.meet()
        unpack(k_ref, natural)
        wide[...] = natural[...].T.astype(jnp.bfloat16)

    def step(t, carry=0):
        at_step(t, coarse_chunks, lambda k: stream.to_col(k).start())
        stream.step(t, coarse_chunks, 1)
        return carry

    step(image)
    conv_image(x_ref.at[0], top_ref.at[0, 0], bottom_ref.at[0, 0], o_ref.at[0], patch, wide)
    borders[image, 0] = o_ref[0, 0]
    borders[image, 1] = o_ref[0, height - 1]
    edges.start(image)

    @pl.when(image == images - 1)
    def _():
        count = borders.shape[0]
        lax.fori_loop(count, max(count, stream.steps(coarse_chunks, 1)), step, 0)
        each(coarse_chunks, stream.drain)
        each(count, edges.drain)


def second_kernel(x_ref, top_ref, bottom_ref, k_ref, o_ref, patch, wide, natural):
    @pl.when(pl.program_id(0) == 0)
    def _():
        unpack(k_ref, natural)
        wide[...] = natural[...].T.astype(jnp.bfloat16)

    conv_image(x_ref.at[0], top_ref.at[0, 0], bottom_ref.at[0, 0], o_ref.at[0], patch, wide)


def conv_specs(x, kernel):
    images, height, channels, width = x.shape
    image = pl.BlockSpec((1, height, channels, width), lambda i: (i, 0, 0, 0))
    top = pl.BlockSpec((1, 1, channels, width), lambda i: (0, i, 0, 0))
    bottom = pl.BlockSpec((1, 1, channels, width), lambda i: (1, i, 0, 0))
    scratch = [
        pltpu.VMEM((height + 2, 3 * channels, width), jnp.bfloat16),
        pltpu.VMEM((channels, 9 * channels), jnp.bfloat16),
        pltpu.VMEM((9 * channels, channels), jnp.float32),
    ]
    whole = pl.BlockSpec(kernel.shape, lambda i: (0, 0, 0, 0))
    return image, [image, top, bottom, whole], scratch


def first_conv(x, rims, kernel, col):
    groups, dp = lax.axis_size("groups"), lax.axis_size("dp")
    images, height, channels, width = x.shape
    chunks, part, fan_out = col.shape
    image, in_specs, scratch = conv_specs(x, kernel)
    any_space = pl.BlockSpec(memory_space=pl.ANY)
    hidden, second, rims = pl.pallas_call(
        functools.partial(first_kernel, groups, dp),
        out_shape=[
            jax.ShapeDtypeStruct(x.shape, x.dtype),
            jax.ShapeDtypeStruct((chunks, 2 * groups, part, fan_out), jnp.bfloat16),
            jax.ShapeDtypeStruct(rims.shape, rims.dtype),
        ],
        grid=(images,),
        in_specs=in_specs + [pl.BlockSpec(col.shape, lambda i: (0, 0, 0))],
        out_specs=[image, any_space, any_space],
        scratch_shapes=scratch
        + [
            pltpu.VMEM((images, 2, channels, width), jnp.bfloat16),
            pltpu.SemaphoreType.DMA((2, 2, images)),
        ]
        + Stream.scratch(chunks, part, fan_out, groups),
        compiler_params=pltpu.CompilerParams(
            collective_id=1, has_side_effects=True, vmem_limit_bytes=56 << 20
        ),
    )(x, rims, rims, kernel, col)
    return hidden, second, rims


def second_conv(x, rims, kernel):
    image, in_specs, scratch = conv_specs(x, kernel)
    return pl.pallas_call(
        second_kernel,
        out_shape=jax.ShapeDtypeStruct(x.shape, x.dtype),
        grid=(x.shape[0],),
        in_specs=in_specs,
        out_specs=image,
        scratch_shapes=scratch,
        compiler_params=pltpu.CompilerParams(vmem_limit_bytes=56 << 20),
    )(x, rims, rims, kernel)


def local(images, kernel_weights, kernel_momentum, kernel_grads, owners):
    x = images.transpose(0, 1, 3, 2)
    kernel, col, rims = spread(kernel_weights, kernel_momentum, kernel_grads, owners, x)
    hidden, kernel, rims = first_conv(x, rims, kernel, col)
    return second_conv(hidden, rims, kernel).transpose(0, 1, 3, 2)


def solution(mesh):
    placed = (
        P("groups", "dp", None, None),
        P("dp", None, None, None, None, None),
        P("dp", None, None, None, None, None),
        P("dp", None, None, None, None, None),
        P(),
    )
    return jax.shard_map(
        local, mesh=mesh, in_specs=placed, out_specs=P("groups", "dp", None, None), check_vma=False
    )
```

```python
import functools

import jax
import jax.numpy as jnp
from jax import lax
from jax.experimental import pallas as pl
from jax.experimental.pallas import tpu as pltpu
from jax.sharding import PartitionSpec as P

momentum_decay = 0.9
learn_rate = 0.5
MESH = pl.DeviceIdType.MESH
fine_chunks = 15
coarse_chunks = 9
pair_hop = 2
hop = 3
slow_hop = 4


class Place:
    def __init__(self, groups, dp):
        self.groups, self.dp, self.last = groups, dp, dp // 4 - 1
        self.group, self.at = lax.axis_index("groups"), lax.axis_index("dp")
        self.z, self.y, self.core = self.at // 4, (self.at // 2) % 2, self.at % 2
        self.mate = self.at + 1 - 2 * self.core
        self.beside = self.at - 1 + 2 * self.core
        self.across = self.at + 2 - 4 * self.y
        self.share = 2 * self.group + self.core
        self.others = [lax.rem(self.group + step, groups) for step in range(1, groups)]
        self.has_beside = (self.beside >= 0) & (self.beside < dp)

    def meet(self):
        barrier = pltpu.get_barrier_semaphore()

        def greet(**where):
            pl.semaphore_signal(barrier, inc=1, device_id=where, device_id_type=MESH)

        greet(dp=self.mate)
        greet(dp=self.across)
        for other in self.others:
            greet(groups=other)
        pl.when(self.has_beside)(lambda: greet(dp=self.beside))
        pl.when(self.z > 0)(lambda: greet(dp=self.at - 4))
        pl.when(self.z < self.last)(lambda: greet(dp=self.at + 4))
        more = [
            jnp.where(there, 1, 0)
            for there in (self.has_beside, self.z > 0, self.z < self.last)
        ]
        pl.semaphore_wait(barrier, 1 + self.groups + sum(more))


def remote(src, dst, sem, k, **where):
    return pltpu.make_async_remote_copy(
        src, dst, sem.at[0, k], sem.at[1, k], device_id=where, device_id_type=MESH
    )


class Stream:
    def __init__(self, place, col, out, col_in, joined, fwd, fwd_in, back, back_in, done, sems):
        self.__dict__.update(place=place, col=col, out=out, col_in=col_in, joined=joined)
        self.__dict__.update(fwd=fwd, fwd_in=fwd_in, back=back, back_in=back_in, done=done)
        self.col_sem, self.fwd_sem, self.back_sem, self.mate_sem = sems[:4]
        self.cross_sem, self.pass_sem, self.keep_sem = sems[4:]

    def to_col(self, k):
        return remote(self.col.at[k], self.col_in.at[k], self.col_sem, k, dp=self.place.across)

    def to_fwd(self, k, up=4):
        return remote(self.fwd.at[k], self.fwd_in.at[k], self.fwd_sem, k, dp=self.place.at + up)

    def to_back(self, k, down=4):
        return remote(self.back.at[k], self.back_in.at[k], self.back_sem, k, dp=self.place.at - down)

    def keep(self, k):
        return pltpu.make_async_copy(
            self.done.at[k], self.out.at[k, self.place.share], self.keep_sem.at[k]
        )

    def to_mate(self, k):
        return remote(
            self.done.at[k], self.out.at[k, self.place.share], self.mate_sem, k, dp=self.place.mate
        )

    def to_cross(self, k, i):
        return remote(
            self.done.at[k], self.out.at[k, self.place.share], self.cross_sem.at[i], k,
            groups=self.place.others[i],
        )

    def to_pass(self, k, i):
        p = self.place
        slot = 2 * lax.rem(p.group + p.groups - 1 - i, p.groups) + p.core
        return remote(self.out.at[k, slot], self.out.at[k, slot], self.pass_sem.at[i], k, dp=p.mate)

    def join_col(self, k):
        self.to_col(k).wait_recv()
        self.joined[k] = self.col[k] + self.col_in[k]

    def go_fwd(self, k):
        p = self.place

        @pl.when(p.z == 0)
        def _():
            self.fwd[k] = self.joined[k]

        @pl.when(p.z > 0)
        def _():
            self.to_fwd(k, -4).wait_recv()
            self.fwd[k] = self.joined[k] + self.fwd_in[k]

        pl.when(p.z < p.last)(lambda: self.to_fwd(k).start())

    def go_back(self, k):
        p = self.place

        @pl.when(p.z == p.last)
        def _():
            self.back[k] = self.joined[k]

        @pl.when(p.z < p.last)
        def _():
            self.to_back(k, -4).wait_recv()
            self.back[k] = self.joined[k] + self.back_in[k]

        pl.when(p.z > 0)(lambda: self.to_back(k).start())

    def finish(self, k):
        p = self.place

        @pl.when(p.z < p.last)
        def _():
            self.done[k] = self.fwd[k] + self.back_in[k]

        @pl.when(p.z == p.last)
        def _():
            self.done[k] = self.fwd[k]

        for i in range(p.groups - 1):
            self.to_cross(k, i).start()
        self.to_mate(k).start()
        self.keep(k).start()

    def pass_on(self, k):
        for i in range(self.place.groups - 1):
            self.to_cross(k, i).wait_recv()
            self.to_pass(k, i).start()

    def steps(self, chunks, hop):
        return chunks + hop * (self.place.last + 2)

    def step(self, t, chunks, hop):
        p = self.place
        at_step(t - hop, chunks, self.join_col)
        at_step(t - hop - p.z * hop, chunks, self.go_fwd)
        at_step(t - hop - (p.last - p.z) * hop, chunks, self.go_back)
        at_step(t - hop - p.last * hop, chunks, self.finish)
        at_step(t - hop - p.last * hop - hop, chunks, self.pass_on)

    def drain(self, k):
        p = self.place
        self.to_col(k).wait_send()
        pl.when(p.z < p.last)(lambda: self.to_fwd(k).wait_send())
        pl.when(p.z > 0)(lambda: self.to_back(k).wait_send())
        self.to_mate(k).wait()
        self.keep(k).wait()
        for i in range(p.groups - 1):
            self.to_cross(k, i).wait_send()
            self.to_pass(k, i).wait()

    @staticmethod
    def scratch(chunks, part, width, groups):
        piece = pltpu.VMEM((chunks, part, width), jnp.bfloat16)
        sems = pltpu.SemaphoreType.DMA((2, chunks))
        many = pltpu.SemaphoreType.DMA((groups - 1, 2, chunks))
        return [piece] * 7 + [sems] * 4 + [many] * 2 + [pltpu.SemaphoreType.DMA((chunks,))]


def half_rows(part):
    return -(-(part // 2) // 8) * 8


def packed_rows(part, width):
    return width // 128 * part + (half_rows(part) if width % 128 else 0)


def packed(v):
    part, width = v.shape
    full, half = width // 128 * 128, half_rows(part)
    blocks = [v[:, i : i + 128] for i in range(0, full, 128)]
    if full < width:
        low, high = v[:half, full:], v[half:, full:]
        if part < 2 * half:
            high = jnp.concatenate(
                [high, jnp.zeros((2 * half - part, width - full), v.dtype)], axis=0
            )
        blocks.append(jnp.concatenate([low, high], axis=1))
    return jnp.concatenate(blocks, axis=0)


def unpack(k_ref, natural):
    chunks, shares, _, _ = k_ref.shape
    depth, width = natural.shape
    part = depth // (chunks * shares)
    full, half = width // 128 * 128, half_rows(part)
    for piece in range(chunks * shares):
        v = k_ref[piece // shares, piece % shares].astype(jnp.float32)
        base = piece * part
        for i in range(full // 128):
            natural[base : base + part, i * 128 : (i + 1) * 128] = v[i * part : (i + 1) * part]
        if full < width:
            rest = v[full // 128 * part :]
            natural[base : base + half, full:] = rest[:, : width - full]
            natural[base + half : base + part, full:] = rest[: part - half, width - full :]


def at_step(k, chunks, what):
    pl.when((k >= 0) & (k < chunks))(lambda: what(k))


def each(chunks, what):
    def body(k, carry):
        what(k)
        return carry

    lax.fori_loop(0, chunks, body, 0)


class Edges:
    def __init__(self, place, first, final, out, sem):
        self.place, self.first, self.final, self.out, self.sem = place, first, final, out, sem

    def down(self, k, to=1):
        return remote(self.final(k), self.out(0, k), self.sem.at[0], k, dp=self.place.at + to)

    def up(self, k, to=1):
        return remote(self.first(k), self.out(1, k), self.sem.at[1], k, dp=self.place.at - to)

    def start(self, k):
        at, dp = self.place.at, self.place.dp
        pl.when(at < dp - 1)(lambda: self.down(k).start())
        pl.when(at > 0)(lambda: self.up(k).start())

    def drain(self, k):
        at, dp = self.place.at, self.place.dp

        @pl.when(at < dp - 1)
        def _():
            self.down(k).wait_send()
            self.up(k, -1).wait_recv()

        @pl.when(at > 0)
        def _():
            self.up(k).wait_send()
            self.down(k, -1).wait_recv()


class Renewal:
    def __init__(self, place, mask, base, state, bufs, col, pair_out, pair_in, load_sem, pair_sem):
        self.place, self.mask, self.base = place, mask, base
        self.state, self.bufs = state, bufs
        self.col, self.pair_out, self.pair_in = col, pair_out, pair_in
        self.load_sem, self.pair_sem = load_sem, pair_sem

    def loads(self, k):
        src = pl.ds(2 * self.place.group, 2)
        return [
            pltpu.make_async_copy(ref.at[self.base + k, src], buf.at[k], self.load_sem.at[i, k])
            for i, (ref, buf) in enumerate(zip(self.state, self.bufs))
        ]

    def start(self, k):
        for copy in self.loads(k):
            copy.start()

    def to_pair(self, k):
        return remote(
            self.pair_out.at[k], self.pair_in.at[k], self.pair_sem, k, dp=self.place.mate
        )

    def renew(self, k):
        for copy in self.loads(k):
            copy.wait()
        w, m, g = self.bufs
        mine = self.mask > 0.5

        def new(c):
            velocity = momentum_decay * m[k, c] + g[k, c].astype(jnp.float32)
            updated = w[k, c].astype(jnp.float32) - learn_rate * velocity
            return packed(jnp.where(mine, updated, 0.0)).astype(jnp.bfloat16)

        self.pair_out[k] = new(1 - self.place.core)
        self.to_pair(k).start()
        self.col[k] = new(self.place.core)

    def join(self, k):
        self.to_pair(k).wait_recv()
        self.col[k] = self.col[k] + self.pair_in[k]

    @staticmethod
    def scratch(chunks, part, width):
        load = lambda dtype: pltpu.VMEM((chunks, 2, part, width), dtype)
        piece = pltpu.VMEM((chunks, packed_rows(part, width), 128), jnp.bfloat16)
        return [load(jnp.bfloat16), load(jnp.float32), load(jnp.bfloat16), piece, piece] + [
            pltpu.SemaphoreType.DMA((3, chunks)),
            pltpu.SemaphoreType.DMA((2, chunks)),
        ]


def spread_kernel(groups, dp, mask_ref, *refs):
    first_state, second_state, x_ref, out_ref, col1_ref, rims_ref = (
        refs[:3], refs[3:6], refs[6], refs[7], refs[8], refs[9],
    )
    scratch = refs[10:]
    place = Place(groups, dp)
    one = Renewal(place, mask_ref[0], 0, first_state, scratch[:3], scratch[14], *scratch[3:7])
    two = Renewal(place, mask_ref[1], coarse_chunks, second_state, scratch[7:10], col1_ref, *scratch[10:14])
    stream = Stream(place, scratch[14], out_ref, *scratch[15:22], scratch[22:29])
    height = x_ref.shape[1]
    edges = Edges(
        place, lambda k: x_ref.at[:, 0], lambda k: x_ref.at[:, height - 1],
        lambda side, k: rims_ref.at[side], scratch[29],
    )
    each(fine_chunks, one.start)
    each(coarse_chunks, two.start)
    place.meet()

    def join(k):
        one.join(k)
        stream.to_col(k).start()

    def step(t, carry):
        at_step(t, fine_chunks, one.renew)
        at_step(t - pair_hop, fine_chunks, join)
        stream.step(t - pair_hop, fine_chunks, hop)
        late = t - fine_chunks - pair_hop
        pl.when(late == 0)(lambda: edges.start(0))
        at_step(late - 1, coarse_chunks, two.renew)
        at_step(late - 1 - pair_hop, coarse_chunks, two.join)
        return carry

    ends = (pair_hop + stream.steps(fine_chunks, hop), fine_chunks + coarse_chunks + 2 * pair_hop + 1)
    lax.fori_loop(0, max(ends), step, 0)

    def drain(k):
        one.to_pair(k).wait_send()
        stream.drain(k)

    each(fine_chunks, drain)
    each(coarse_chunks, lambda k: two.to_pair(k).wait_send())
    edges.drain(0)


def spread(kernel_weights, kernel_momentum, kernel_grads, owners, x):
    groups, dp = lax.axis_size("groups"), lax.axis_size("dp")
    _, _, rows, columns, fan_in, fan_out = kernel_weights.shape
    images, _, channels, width = x.shape
    shares, depth = 2 * groups, rows * columns * fan_in
    mine = (owners == lax.axis_index("dp")).astype(jnp.float32)
    mask = jnp.broadcast_to(mine[:, None, None], (2, 1, fan_out))
    state = (kernel_weights, kernel_momentum, kernel_grads)

    def cut(chunks):
        return [a.reshape(2 * chunks, shares, -1, fan_out) for a in state]

    fine, coarse = depth // fine_chunks // shares, depth // coarse_chunks // shares
    fine_rows, coarse_rows = packed_rows(fine, fan_out), packed_rows(coarse, fan_out)
    any_space = pl.BlockSpec(memory_space=pl.ANY)
    vmem = pl.BlockSpec(memory_space=pltpu.VMEM)
    kernel, col, rims = pl.pallas_call(
        functools.partial(spread_kernel, groups, dp),
        out_shape=[
            jax.ShapeDtypeStruct((fine_chunks, shares, fine_rows, 128), jnp.bfloat16),
            jax.ShapeDtypeStruct((coarse_chunks, coarse_rows, 128), jnp.bfloat16),
            jax.ShapeDtypeStruct((2, images, channels, width), jnp.bfloat16),
        ],
        in_specs=[vmem] + [any_space] * 7,
        out_specs=[vmem, vmem, any_space],
        scratch_shapes=Renewal.scratch(fine_chunks, fine, fan_out)
        + Renewal.scratch(coarse_chunks, coarse, fan_out)
        + [pltpu.VMEM((fine_chunks, fine_rows, 128), jnp.bfloat16)]
        + Stream.scratch(fine_chunks, fine_rows, 128, groups)
        + [pltpu.SemaphoreType.DMA((2, 2, 1))],
        compiler_params=pltpu.CompilerParams(
            collective_id=0, has_side_effects=True, vmem_limit_bytes=56 << 20
        ),
    )(mask, *cut(fine_chunks), *cut(coarse_chunks), x)
    return kernel, col, rims


def silu(v):
    return v / (1.0 + jnp.exp(-v))


def conv_image(x_ref, top_ref, bottom_ref, o_ref, patch, wide, between=lambda row: None):
    height, channels, width = x_ref.shape
    at = lax.axis_index("dp")
    column = lax.broadcasted_iota(jnp.int32, (1, width), 1)

    def build(row):
        if row == 0:
            v = jnp.where(at > 0, top_ref[...].astype(jnp.float32), 0.0)
        elif row == height + 1:
            v = jnp.where(at < lax.axis_size("dp") - 1, bottom_ref[...].astype(jnp.float32), 0.0)
        else:
            v = x_ref[row - 1]
        a = silu(v.astype(jnp.float32))
        before = jnp.where(column == 0, 0.0, pltpu.roll(a, 1, 1))
        after = jnp.where(column == width - 1, 0.0, pltpu.roll(a, width - 1, 1))
        for dc, part in enumerate((before, a, after)):
            patch[row, dc * channels : (dc + 1) * channels] = part.astype(jnp.bfloat16)

    built = 0
    for row in range(0, height, 2):
        between(row)
        while built < row + 4:
            build(built)
            built += 1
        rhs = jnp.concatenate(
            [
                jnp.concatenate([patch[row + dr], patch[row + dr + 1]], axis=1)
                for dr in range(3)
            ],
            axis=0,
        )
        acc = jnp.dot(wide[...], rhs, preferred_element_type=jnp.float32)
        for i in range(2):
            x = x_ref[row + i].astype(jnp.float32)
            o_ref[row + i] = (x + acc[:, i * width : (i + 1) * width]).astype(o_ref.dtype)


def first_kernel(groups, dp, x_ref, top_ref, bottom_ref, k_ref, col_ref, o_ref, out_ref, rims_ref,
                 patch, wide, natural, borders, edge_sem, *scratch):
    place = Place(groups, dp)
    image, images = pl.program_id(0), pl.num_programs(0)
    height = x_ref.shape[1]
    stream = Stream(place, col_ref, out_ref, *scratch[:7], scratch[7:])
    edges = Edges(
        place, lambda k: borders.at[k, 0], lambda k: borders.at[k, 1],
        lambda side, k: rims_ref.at[side, k], edge_sem,
    )

    @pl.when(image == 0)
    def _():
        place.meet()
        unpack(k_ref, natural)
        wide[...] = natural[...].T.astype(jnp.bfloat16)

    def step(t, carry=0):
        at_step(t, coarse_chunks, lambda k: stream.to_col(k).start())
        stream.step(t, coarse_chunks, slow_hop)
        return carry

    def between(row):
        if row % (height // 2) == 0:
            now = 4 * image + row // (height // 2) * 2
            step(now)
            step(now + 1)

    conv_image(x_ref.at[0], top_ref.at[0, 0], bottom_ref.at[0, 0], o_ref.at[0], patch, wide, between)
    borders[image, 0] = o_ref[0, 0]
    borders[image, 1] = o_ref[0, height - 1]
    edges.start(image)

    @pl.when(image == images - 1)
    def _():
        count = borders.shape[0]
        lax.fori_loop(4 * count, max(4 * count, stream.steps(coarse_chunks, slow_hop)), step, 0)
        each(coarse_chunks, stream.drain)
        each(count, edges.drain)


def second_kernel(x_ref, top_ref, bottom_ref, k_ref, o_ref, patch, wide, natural):
    @pl.when(pl.program_id(0) == 0)
    def _():
        unpack(k_ref, natural)
        wide[...] = natural[...].T.astype(jnp.bfloat16)

    conv_image(x_ref.at[0], top_ref.at[0, 0], bottom_ref.at[0, 0], o_ref.at[0], patch, wide)


def conv_specs(x, kernel):
    images, height, channels, width = x.shape
    image = pl.BlockSpec((1, height, channels, width), lambda i: (i, 0, 0, 0))
    top = pl.BlockSpec((1, 1, channels, width), lambda i: (0, i, 0, 0))
    bottom = pl.BlockSpec((1, 1, channels, width), lambda i: (1, i, 0, 0))
    scratch = [
        pltpu.VMEM((height + 2, 3 * channels, width), jnp.bfloat16),
        pltpu.VMEM((channels, 9 * channels), jnp.bfloat16),
        pltpu.VMEM((9 * channels, channels), jnp.float32),
    ]
    whole = pl.BlockSpec(kernel.shape, lambda i: (0, 0, 0, 0))
    return image, [image, top, bottom, whole], scratch


def first_conv(x, rims, kernel, col):
    groups, dp = lax.axis_size("groups"), lax.axis_size("dp")
    images, height, channels, width = x.shape
    chunks, part, fan_out = col.shape
    image, in_specs, scratch = conv_specs(x, kernel)
    any_space = pl.BlockSpec(memory_space=pl.ANY)
    hidden, second, rims = pl.pallas_call(
        functools.partial(first_kernel, groups, dp),
        out_shape=[
            jax.ShapeDtypeStruct(x.shape, x.dtype),
            jax.ShapeDtypeStruct((chunks, 2 * groups, part, fan_out), jnp.bfloat16),
            jax.ShapeDtypeStruct(rims.shape, rims.dtype),
        ],
        grid=(images,),
        in_specs=in_specs + [pl.BlockSpec(col.shape, lambda i: (0, 0, 0))],
        out_specs=[image, any_space, any_space],
        scratch_shapes=scratch
        + [
            pltpu.VMEM((images, 2, channels, width), jnp.bfloat16),
            pltpu.SemaphoreType.DMA((2, 2, images)),
        ]
        + Stream.scratch(chunks, part, fan_out, groups),
        compiler_params=pltpu.CompilerParams(
            collective_id=1, has_side_effects=True, vmem_limit_bytes=56 << 20
        ),
    )(x, rims, rims, kernel, col)
    return hidden, second, rims


def second_conv(x, rims, kernel):
    image, in_specs, scratch = conv_specs(x, kernel)
    return pl.pallas_call(
        second_kernel,
        out_shape=jax.ShapeDtypeStruct(x.shape, x.dtype),
        grid=(x.shape[0],),
        in_specs=in_specs,
        out_specs=image,
        scratch_shapes=scratch,
        compiler_params=pltpu.CompilerParams(vmem_limit_bytes=56 << 20),
    )(x, rims, rims, kernel)


def local(images, kernel_weights, kernel_momentum, kernel_grads, owners):
    x = images.transpose(0, 1, 3, 2)
    kernel, col, rims = spread(kernel_weights, kernel_momentum, kernel_grads, owners, x)
    hidden, kernel, rims = first_conv(x, rims, kernel, col)
    return second_conv(hidden, rims, kernel).transpose(0, 1, 3, 2)


def solution(mesh):
    placed = (
        P("groups", "dp", None, None),
        P("dp", None, None, None, None, None),
        P("dp", None, None, None, None, None),
        P("dp", None, None, None, None, None),
        P(),
    )
    return jax.shard_map(
        local, mesh=mesh, in_specs=placed, out_specs=P("groups", "dp", None, None), check_vma=False
    )
```
